32 devices in a mesh: theta: 16 (over z, x, core), gz: 2 (over y).
Axes of the slice: x: 2, y: 2, z: 4, core: 2. Of those that a mesh axis runs over, the one named last changes fastest.
Arguments:
- field: float32 [16, 1024, 1024], P('gz', 'theta'), parts along dimension 0, may hold values from -6 to 6
- courant: float32 [1024], replicated, may hold values from 0.2 to 0.8
Outputs:
- advanced: float32 [16, 1024, 1024], P('gz', 'theta'), parts along dimension 0
The draws below stay inside these ranges and needn't reach their ends.
There are 2 independent parts, one for each index of `gz`. The reference program is written for one: setup_inputs(seed, part) draws one part's arguments, and reference() takes and returns one part's arrays. A program takes and returns all parts, laid end to end along the dimension named above; an argument that names none is the same for every part. Nothing has to cross between parts.
All inputs are finite; a program needn't handle non-finite values.
Results may differ from the reference program's by a relative error of at most 0.00007.
Values sent between devices are 32-bit elements; how exact they have to be, the bound alone decides.
A program may use at most 128 MiB of HBM per device.

```python
import math
import jax
import jax.numpy as jnp
from jax import lax

NR = 1024
H = 8
NTH = 1024


def shard_levels(key, dims, shards, least, high):
    gain, own = 1.0, jax.random.fold_in(key, 6)
    for axis_at, blocks in shards:
        steps = jnp.exp(jax.random.uniform(jax.random.fold_in(own, axis_at), (blocks,), jnp.float32, least / len(shards), high / len(shards)))
        gain = gain * jnp.repeat(steps, dims[axis_at] // blocks).reshape([-1 if axis == axis_at else 1 for axis in range(len(dims))])
    return gain


def noise(own_key, dims, deviation, most, split=(), kind=jnp.bfloat16):
    factor_of = shard_levels(own_key, dims, split, -0.22, 0.18) if split else 1.0
    entries = jax.random.normal(own_key, dims, jnp.float32) * deviation * factor_of
    return jnp.minimum(jnp.maximum(entries, -most), most).astype(kind)


def setup_inputs(seed: int = 0, part: int = 0) -> dict:
    streams_of = jax.random.split(jax.random.key(seed), 3)
    own_keys = jax.random.split(jax.random.fold_in(streams_of[2], part), 3)
    return {
        "field": noise(own_keys[0], (H, NTH, NR), 1.0, 6.0, ((1, 16),), jnp.float32),
        "courant": jnp.clip(jnp.exp(jax.random.uniform(streams_of[1], (NR,), jnp.float32, math.log(0.2), math.log(0.8))), 0.2, 0.8),
    }


stencil_weights = (4.0 / 5.0, -1.0 / 5.0, 4.0 / 105.0, -1.0 / 280.0)
radial_step = 0.2


def diameter_blocks(radial_count):
    intervals = 2 * radial_count - 1
    row_index = jnp.arange(radial_count, dtype=jnp.int32)[:, None]
    col_index = jnp.arange(2 * radial_count, dtype=jnp.int32)[None, :]
    angle_unit = math.pi / (2 * intervals)
    summed = (row_index + col_index).astype(jnp.float32) * angle_unit
    differ = (row_index - col_index).astype(jnp.float32) * angle_unit
    spacing = -2.0 * jnp.sin(summed) * jnp.sin(differ)
    same = row_index == col_index
    row_factor = jnp.where(row_index == 0, 2.0, 1.0).astype(jnp.float32)
    col_factor = jnp.where((col_index == 0) | (col_index == intervals), 2.0, 1.0).astype(jnp.float32)
    parity = jnp.where((row_index + col_index) % 2 == 0, 1.0, -1.0).astype(jnp.float32)
    safe_spacing = jnp.where(same, 1.0, spacing)
    offdiag = jnp.where(same, 0.0, row_factor / col_factor * parity / safe_spacing)
    matrix = offdiag - jnp.where(same, jnp.sum(offdiag, axis=1, keepdims=True), 0.0)
    near = matrix[:, :radial_count].T
    far = matrix[:, radial_count:][:, ::-1].T
    return near, far


def radial_weight(radial_count):
    intervals = 2 * radial_count - 1
    angles = jnp.arange(radial_count, dtype=jnp.int32).astype(jnp.float32) * (math.pi / intervals)
    return jnp.sin(angles) ** 2


def azimuth_difference(extended, rows):
    total = jnp.zeros((extended.shape[0], rows, extended.shape[2]), jnp.float32)
    for offset in range(1, 5):
        total = total + stencil_weights[offset - 1] * (extended[:, 4 + offset:4 + offset + rows] - extended[:, 4 - offset:4 - offset + rows])
    return total


def reference(field, courant):
    near, far = diameter_blocks(NR)
    weight = radial_weight(NR)
    tau = radial_step / (2 * NR - 1)

    def section_rate(state):
        padded = jnp.concatenate([state[:, -4:], state, state[:, :4]], axis=1)
        azimuth = azimuth_difference(padded, NTH)
        opposite = jnp.roll(state, NTH // 2, axis=1)
        deriv = jnp.dot(state.reshape(-1, NR), near, precision=lax.Precision.HIGHEST) + jnp.dot(opposite.reshape(-1, NR), far, precision=lax.Precision.HIGHEST)
        deriv = deriv.reshape(state.shape)
        return -courant * azimuth - tau * weight * state * deriv

    first = field + section_rate(field)
    second = 0.75 * field + 0.25 * (first + section_rate(first))
    return field / 3.0 + (2.0 / 3.0) * (second + section_rate(second))
```

```python
import functools

import jax
import jax.numpy as jnp
import numpy as np
from jax import lax
from jax.experimental import pallas as pl
from jax.experimental.pallas import tpu as pltpu
from jax.sharding import PartitionSpec as P

stencil_weights = (4.0 / 5.0, -1.0 / 5.0, 4.0 / 105.0, -1.0 / 280.0)
radial_step = 0.2
PLANES = 4
PAD = 8
TILE = 256
MESH = pl.DeviceIdType.MESH


def radial_tables(radial_count):
    last = 2 * radial_count - 1
    i = np.arange(radial_count)
    l = np.arange(last + 1)
    unit = np.pi / (2 * last)
    x = np.cos(2 * unit * i)
    high = x.astype(np.float32)
    low = (x - high.astype(np.float64)).astype(np.float32)
    gap = -2.0 * np.sin(unit * (i[:, None] + l)) * np.sin(unit * (i[:, None] - l))
    same = i[:, None] == l
    ci = np.where(i == 0, 2.0, 1.0)
    cl = np.where((l == 0) | (l == last), 2.0, 1.0)
    sign = np.where((i[:, None] + l) % 2 == 0, 1.0, -1.0)
    off = np.where(same, 0.0, ci[:, None] / cl * sign / np.where(same, 1.0, gap))
    diagonal = -off.sum(axis=1)
    mirror = off[i, last - i]
    scale = 0.5 * radial_step / last * np.sin(2 * unit * i) ** 2
    column = scale * ci * np.where(i % 2 == 0, 1.0, -1.0)
    row = np.where(i % 2 == 0, 1.0, -1.0) / ci
    even = scale * (diagonal + mirror)
    odd = scale * (diagonal - mirror)
    return np.stack([high, low, column, row, even, odd, 0 * x, 0 * x]).astype(np.float32)


def build_matrices(table, mats, radial_count):
    blk = 128

    @pl.loop(0, radial_count // blk)
    def _(lb):
        l0 = pl.multiple_of(lb * blk, blk)

        def down(k):
            return jnp.transpose(jnp.broadcast_to(table[k : k + 1, pl.ds(l0, blk)], (blk, blk)))

        high, low, row = down(0), down(1), down(3)
        rows = lax.broadcasted_iota(jnp.int32, (blk, blk), 0) + l0

        @pl.loop(0, radial_count // blk)
        def _(jb):
            j0 = pl.multiple_of(jb * blk, blk)
            cols = pl.ds(j0, blk)
            same = rows == lax.broadcasted_iota(jnp.int32, (blk, blk), 1) + j0
            near = (table[0:1, cols] - high) + (table[1:2, cols] - low)
            far = table[0:1, cols] + high
            near = 1.0 / jnp.where(same, 1.0, near)
            far = 1.0 / far
            factor = table[2:3, cols] * row
            even = jnp.where(same, table[4:5, cols], factor * (near - far))
            odd = jnp.where(same, table[5:6, cols], factor * (near + far))
            for k, m in enumerate((even, odd)):
                head = m.astype(jnp.bfloat16)
                mats[2 * k, pl.ds(l0, blk), cols] = head
                mats[2 * k + 1, pl.ds(l0, blk), cols] = (m - head.astype(jnp.float32)).astype(jnp.bfloat16)


def kernel(
    size,
    field,
    courant,
    table,
    out,
    state,
    mats,
    split,
    deriv,
    edge_out,
    edge_in,
    own_sem,
    in_send,
    in_recv,
    out_send,
    out_recv,
    edge_send,
    edge_recv,
):
    ring = size // PLANES
    heights, rows, radial_count = field.shape
    per = heights // PLANES
    half = PLANES // 2
    me = lax.axis_index("theta")
    g = lax.div(me, ring)
    q = lax.rem(me, ring)
    right = g * ring + lax.rem(q + 1, ring)
    left = g * ring + lax.rem(q + ring - 1, ring)
    high_bit, low_bit = lax.div(g, 2), lax.rem(g, 2)

    def partner(m):
        a, b = m // 2, m % 2
        return 2 * (high_bit + a - 2 * a * high_bit) + (low_bit + b - 2 * b * low_bit)

    order = (3, 2, 1)
    others = [partner(m) for m in order]
    body = pl.ds(PAD, rows)

    barrier = pltpu.get_barrier_semaphore()
    for d in [o * ring + q for o in others] + [right, left]:
        pl.semaphore_signal(barrier, inc=1, device_id={"theta": d}, device_id_type=MESH)
    pl.semaphore_wait(barrier, len(others) + 2)

    def incoming(h, k):
        o = others[k]
        return pltpu.make_async_remote_copy(
            field.at[o * per + h],
            state.at[0, h, g, body],
            in_send.at[h, k],
            in_recv.at[h, k],
            device_id={"theta": o * ring + q},
            device_id_type=MESH,
        )

    def outgoing(h, k):
        o = others[k]
        return pltpu.make_async_remote_copy(
            state.at[3, h, o, body],
            out.at[g * per + h],
            out_send.at[h, k],
            out_recv.at[h, k],
            device_id={"theta": o * ring + q},
            device_id_type=MESH,
        )

    def own_in(h):
        return pltpu.make_async_copy(field.at[g * per + h], state.at[0, h, g, body], own_sem.at[0, h])

    def own_out(h):
        return pltpu.make_async_copy(state.at[3, h, g, body], out.at[g * per + h], own_sem.at[1, h])

    def edge(sec, h, way):
        return pltpu.make_async_remote_copy(
            edge_out.at[sec, h, way],
            edge_in.at[sec, h, way],
            edge_send.at[sec, h, way],
            edge_recv.at[sec, h, way],
            device_id={"theta": right if way == 0 else left},
            device_id_type=MESH,
        )

    for h in range(per):
        for k in range(len(order)):
            incoming(h, k).start()
        own_in(h).start()

    build_matrices(table, mats, radial_count)

    wrap_right = lax.div(q, ring - 1)
    wrap_left = lax.div(ring - 1 - q, ring - 1)
    pair_rows = half * rows
    tiles = radial_count // TILE

    @pl.loop(0, per * 3)
    def _(step):
        h = lax.div(step, 3)
        sec = lax.rem(step, 3)

        @pl.when(sec == 0)
        def _():
            own_in(h).wait()
            for k in range(len(order)):
                incoming(h, k).wait_recv()

        for s in range(PLANES):
            src = lax.rem(s + PLANES - wrap_right, PLANES)
            edge_out[sec, h, 0, 4 * s : 4 * s + 4] = state[sec, h, src, PAD + rows - 4 : PAD + rows]
            src = lax.rem(s + wrap_left, PLANES)
            edge_out[sec, h, 1, 4 * s : 4 * s + 4] = state[sec, h, src, PAD : PAD + 4]
        edge(sec, h, 0).start()
        edge(sec, h, 1).start()

        @pl.loop(0, tiles)
        def _(c):
            cols = pl.ds(pl.multiple_of(c * TILE, TILE), TILE)
            for s in range(half):
                a = state[sec, h, s, body, cols]
                b = state[sec, h, s + half, body, cols]
                for k, w in enumerate((a + b, a - b)):
                    head = w.astype(jnp.bfloat16)
                    tail = (w - head.astype(jnp.float32)).astype(jnp.bfloat16)
                    split[k, s * rows : (s + 1) * rows, cols] = head
                    split[k, pair_rows + s * rows : pair_rows + (s + 1) * rows, cols] = tail

        @pl.loop(0, tiles)
        def _(c):
            cols = pl.ds(pl.multiple_of(c * TILE, TILE), TILE)
            parts = []
            for k in range(2):
                both = jnp.dot(split[k], mats[2 * k, :, cols], preferred_element_type=jnp.float32)
                rest = jnp.dot(
                    split[k, :pair_rows], mats[2 * k + 1, :, cols], preferred_element_type=jnp.float32
                )
                parts.append(both[:pair_rows] + (both[pair_rows:] + rest))
            deriv[0, :, cols] = parts[0] + parts[1]
            deriv[1, :, cols] = parts[0] - parts[1]

        edge(sec, h, 0).wait()
        edge(sec, h, 1).wait()
        for s in range(PLANES):
            state[sec, h, s, PAD - 4 : PAD] = edge_in[sec, h, 0, 4 * s : 4 * s + 4]
            state[sec, h, s, PAD + rows : PAD + rows + 4] = edge_in[sec, h, 1, 4 * s : 4 * s + 4]

        start_part = jnp.where(sec == 0, 0.0, jnp.where(sec == 1, 0.75, 1.0 / 3.0)).astype(jnp.float32)
        step_part = jnp.where(sec == 0, 1.0, jnp.where(sec == 1, 0.25, 2.0 / 3.0)).astype(jnp.float32)

        @pl.loop(0, tiles)
        def _(c):
            cols = pl.ds(pl.multiple_of(c * TILE, TILE), TILE)
            speed = courant[:, cols]
            for s in range(PLANES):
                total = jnp.zeros((rows, TILE), jnp.float32)
                for o in range(1, 5):
                    total = total + stencil_weights[o - 1] * (
                        state[sec, h, s, PAD + o : PAD + o + rows, cols]
                        - state[sec, h, s, PAD - o : PAD - o + rows, cols]
                    )
                now = state[sec, h, s, body, cols]
                d = deriv[s // half, (s % half) * rows : (s % half + 1) * rows, cols]
                moved = now - speed * total - now * d
                state[sec + 1, h, s, body, cols] = start_part * state[0, h, s, body, cols] + step_part * moved

        @pl.when(sec == 2)
        def _():
            for k in range(len(order)):
                outgoing(h, k).start()
            own_out(h).start()

    for h in range(per):
        for k in range(len(order)):
            incoming(h, k).wait_send()
        own_out(h).wait()
    for h in range(per):
        for k in range(len(order)):
            outgoing(h, k).wait()


def body(size, field, courant):
    heights, rows, radial_count = field.shape
    per = heights // PLANES
    table = jnp.asarray(radial_tables(radial_count))
    f32, bf16 = jnp.float32, jnp.bfloat16
    dma = pltpu.SemaphoreType.DMA
    vmem = pl.BlockSpec(memory_space=pltpu.VMEM)
    anywhere = pl.BlockSpec(memory_space=pl.ANY)
    return pl.pallas_call(
        functools.partial(kernel, size),
        out_shape=jax.ShapeDtypeStruct(field.shape, f32),
        in_specs=[anywhere, vmem, vmem],
        out_specs=anywhere,
        scratch_shapes=[
            pltpu.VMEM((4, per, PLANES, rows + 2 * PAD, radial_count), f32),
            pltpu.VMEM((4, radial_count, radial_count), bf16),
            pltpu.VMEM((2, PLANES * rows, radial_count), bf16),
            pltpu.VMEM((2, PLANES // 2 * rows, radial_count), f32),
            pltpu.VMEM((3, per, 2, 4 * PLANES, radial_count), f32),
            pltpu.VMEM((3, per, 2, 4 * PLANES, radial_count), f32),
            dma((2, per)),
            dma((per, PLANES - 1)),
            dma((per, PLANES - 1)),
            dma((per, PLANES - 1)),
            dma((per, PLANES - 1)),
            dma((3, per, 2)),
            dma((3, per, 2)),
        ],
        compiler_params=pltpu.CompilerParams(
            collective_id=0, has_side_effects=True, vmem_limit_bytes=56 << 20
        ),
    )(field, courant.reshape(1, -1), table)


def solution(mesh):
    size = mesh.shape["theta"]
    return jax.shard_map(
        functools.partial(body, size),
        mesh=mesh,
        in_specs=(P("gz", "theta", None), P()),
        out_specs=P("gz", "theta", None),
        check_vma=False,
    )
```

```python
import functools

import jax
import jax.numpy as jnp
import numpy as np
from jax import lax
from jax.experimental import pallas as pl
from jax.experimental.pallas import tpu as pltpu
from jax.sharding import PartitionSpec as P

stencil_weights = (4.0 / 5.0, -1.0 / 5.0, 4.0 / 105.0, -1.0 / 280.0)
radial_step = 0.2
PLANES = 4
PAD = 8
TILE = 256
MESH = pl.DeviceIdType.MESH


def radial_tables(radial_count):
    last = 2 * radial_count - 1
    i = np.arange(radial_count)
    l = np.arange(last + 1)
    unit = np.pi / (2 * last)
    x = np.cos(2 * unit * i)
    high = x.astype(np.float32)
    low = (x - high.astype(np.float64)).astype(np.float32)
    gap = -2.0 * np.sin(unit * (i[:, None] + l)) * np.sin(unit * (i[:, None] - l))
    same = i[:, None] == l
    ci = np.where(i == 0, 2.0, 1.0)
    cl = np.where((l == 0) | (l == last), 2.0, 1.0)
    sign = np.where((i[:, None] + l) % 2 == 0, 1.0, -1.0)
    off = np.where(same, 0.0, ci[:, None] / cl * sign / np.where(same, 1.0, gap))
    diagonal = -off.sum(axis=1)
    mirror = off[i, last - i]
    scale = 0.5 * radial_step / last * np.sin(2 * unit * i) ** 2
    column = scale * ci * np.where(i % 2 == 0, 1.0, -1.0)
    row = np.where(i % 2 == 0, 1.0, -1.0) / ci
    even = scale * (diagonal + mirror)
    odd = scale * (diagonal - mirror)
    return np.stack([high, low, column, row, even, odd, 0 * x, 0 * x]).astype(np.float32)


def build_matrices(table, mats, radial_count):
    blk = 128

    @pl.loop(0, radial_count // blk)
    def _(lb):
        l0 = pl.multiple_of(lb * blk, blk)

        def down(k):
            return jnp.transpose(jnp.broadcast_to(table[k : k + 1, pl.ds(l0, blk)], (blk, blk)))

        high, low, row = down(0), down(1), down(3)
        rows = lax.broadcasted_iota(jnp.int32, (blk, blk), 0) + l0

        @pl.loop(0, radial_count // blk)
        def _(jb):
            j0 = pl.multiple_of(jb * blk, blk)
            cols = pl.ds(j0, blk)
            same = rows == lax.broadcasted_iota(jnp.int32, (blk, blk), 1) + j0
            near = (table[0:1, cols] - high) + (table[1:2, cols] - low)
            far = table[0:1, cols] + high
            near = 1.0 / jnp.where(same, 1.0, near)
            far = 1.0 / far
            factor = table[2:3, cols] * row
            even = jnp.where(same, table[4:5, cols], factor * (near - far))
            odd = jnp.where(same, table[5:6, cols], factor * (near + far))
            for k, m in enumerate((even, odd)):
                head = m.astype(jnp.bfloat16)
                mats[2 * k, pl.ds(l0, blk), cols] = head
                mats[2 * k + 1, pl.ds(l0, blk), cols] = (m - head.astype(jnp.float32)).astype(jnp.bfloat16)


def kernel(
    size,
    field,
    courant_in,
    table_in,
    out,
    courant,
    table,
    state,
    mats,
    split,
    deriv,
    edge_out,
    edge_in,
    table_sem,
    own_sem,
    in_send,
    in_recv,
    out_send,
    out_recv,
    edge_send,
    edge_recv,
):
    ring = size // PLANES
    heights, rows, radial_count = field.shape
    per = heights // PLANES
    half = PLANES // 2
    me = lax.axis_index("theta")
    g = lax.div(me, ring)
    q = lax.rem(me, ring)
    right = g * ring + lax.rem(q + 1, ring)
    left = g * ring + lax.rem(q + ring - 1, ring)
    high_bit, low_bit = lax.div(g, 2), lax.rem(g, 2)

    def partner(m):
        a, b = m // 2, m % 2
        return 2 * (high_bit + a - 2 * a * high_bit) + (low_bit + b - 2 * b * low_bit)

    order = (3, 2, 1)
    others = [partner(m) for m in order]
    body = pl.ds(PAD, rows)

    barrier = pltpu.get_barrier_semaphore()
    for d in [o * ring + q for o in others] + [right, left]:
        pl.semaphore_signal(barrier, inc=1, device_id={"theta": d}, device_id_type=MESH)
    pl.semaphore_wait(barrier, len(others) + 2)

    def incoming(h, k):
        o = others[k]
        return pltpu.make_async_remote_copy(
            field.at[o * per + h],
            state.at[0, h, g, body],
            in_send.at[h, k],
            in_recv.at[h, k],
            device_id={"theta": o * ring + q},
            device_id_type=MESH,
        )

    def outgoing(h, k):
        o = others[k]
        return pltpu.make_async_remote_copy(
            state.at[3, h, o, body],
            out.at[g * per + h],
            out_send.at[h, k],
            out_recv.at[h, k],
            device_id={"theta": o * ring + q},
            device_id_type=MESH,
        )

    def own_in(h):
        return pltpu.make_async_copy(field.at[g * per + h], state.at[0, h, g, body], own_sem.at[0, h])

    def own_out(h):
        return pltpu.make_async_copy(state.at[3, h, g, body], out.at[g * per + h], own_sem.at[1, h])

    def edge(sec, h, way):
        return pltpu.make_async_remote_copy(
            edge_out.at[sec, h, way],
            edge_in.at[sec, h, way],
            edge_send.at[sec, h, way],
            edge_recv.at[sec, h, way],
            device_id={"theta": right if way == 0 else left},
            device_id_type=MESH,
        )

    for h in range(per):
        for k in range(len(order)):
            incoming(h, k).start()
        own_in(h).start()

    loads = [
        pltpu.make_async_copy(table_in, table, table_sem.at[0]),
        pltpu.make_async_copy(courant_in, courant, table_sem.at[1]),
    ]
    for load in loads:
        load.start()
    for load in loads:
        load.wait()
    build_matrices(table, mats, radial_count)

    wrap_right = lax.div(q, ring - 1)
    wrap_left = lax.div(ring - 1 - q, ring - 1)
    pair_rows = half * rows
    tiles = radial_count // TILE

    @pl.loop(0, per * 3)
    def _(step):
        h = lax.div(step, 3)
        sec = lax.rem(step, 3)

        @pl.when(sec == 0)
        def _():
            own_in(h).wait()
            for k in range(len(order)):
                incoming(h, k).wait_recv()

        for s in range(PLANES):
            src = lax.rem(s + PLANES - wrap_right, PLANES)
            edge_out[sec, h, 0, 4 * s : 4 * s + 4] = state[sec, h, src, PAD + rows - 4 : PAD + rows]
            src = lax.rem(s + wrap_left, PLANES)
            edge_out[sec, h, 1, 4 * s : 4 * s + 4] = state[sec, h, src, PAD : PAD + 4]
        edge(sec, h, 0).start()
        edge(sec, h, 1).start()

        @pl.loop(0, tiles)
        def _(c):
            cols = pl.ds(pl.multiple_of(c * TILE, TILE), TILE)
            for s in range(half):
                a = state[sec, h, s, body, cols]
                b = state[sec, h, s + half, body, cols]
                for k, w in enumerate((a + b, a - b)):
                    head = w.astype(jnp.bfloat16)
                    tail = (w - head.astype(jnp.float32)).astype(jnp.bfloat16)
                    split[k, s * rows : (s + 1) * rows, cols] = head
                    split[k, pair_rows + s * rows : pair_rows + (s + 1) * rows, cols] = tail

        @pl.loop(0, tiles)
        def _(c):
            cols = pl.ds(pl.multiple_of(c * TILE, TILE), TILE)
            parts = []
            for k in range(2):
                both = jnp.dot(split[k], mats[2 * k, :, cols], preferred_element_type=jnp.float32)
                rest = jnp.dot(
                    split[k, :pair_rows], mats[2 * k + 1, :, cols], preferred_element_type=jnp.float32
                )
                parts.append(both[:pair_rows] + (both[pair_rows:] + rest))
            deriv[0, :, cols] = parts[0] + parts[1]
            deriv[1, :, cols] = parts[0] - parts[1]

        edge(sec, h, 0).wait()
        edge(sec, h, 1).wait()
        for s in range(PLANES):
            state[sec, h, s, PAD - 4 : PAD] = edge_in[sec, h, 0, 4 * s : 4 * s + 4]
            state[sec, h, s, PAD + rows : PAD + rows + 4] = edge_in[sec, h, 1, 4 * s : 4 * s + 4]

        start_part = jnp.where(sec == 0, 0.0, jnp.where(sec == 1, 0.75, 1.0 / 3.0)).astype(jnp.float32)
        step_part = jnp.where(sec == 0, 1.0, jnp.where(sec == 1, 0.25, 2.0 / 3.0)).astype(jnp.float32)

        @pl.loop(0, tiles)
        def _(c):
            cols = pl.ds(pl.multiple_of(c * TILE, TILE), TILE)
            speed = courant[:, cols]
            for s in range(PLANES):
                total = jnp.zeros((rows, TILE), jnp.float32)
                for o in range(1, 5):
                    total = total + stencil_weights[o - 1] * (
                        state[sec, h, s, PAD + o : PAD + o + rows, cols]
                        - state[sec, h, s, PAD - o : PAD - o + rows, cols]
                    )
                now = state[sec, h, s, body, cols]
                d = deriv[s // half, (s % half) * rows : (s % half + 1) * rows, cols]
                moved = now - speed * total - now * d
                state[sec + 1, h, s, body, cols] = start_part * state[0, h, s, body, cols] + step_part * moved

        @pl.when(sec == 2)
        def _():
            for k in (1, 2, 0):
                outgoing(h, k).start()
            own_out(h).start()

    for h in range(per):
        for k in range(len(order)):
            incoming(h, k).wait_send()
        own_out(h).wait()
    for h in range(per):
        for k in range(len(order)):
            outgoing(h, k).wait()


def body(size, field, courant):
    heights, rows, radial_count = field.shape
    per = heights // PLANES
    table = jnp.asarray(radial_tables(radial_count))
    f32, bf16 = jnp.float32, jnp.bfloat16
    dma = pltpu.SemaphoreType.DMA
    anywhere = pl.BlockSpec(memory_space=pl.ANY)
    return pl.pallas_call(
        functools.partial(kernel, size),
        out_shape=pltpu.VMEM(field.shape, f32),
        in_specs=[anywhere] * 3,
        out_specs=pl.BlockSpec(memory_space=pltpu.VMEM),
        scratch_shapes=[
            pltpu.VMEM((1, radial_count), f32),
            pltpu.VMEM(table.shape, f32),
            pltpu.VMEM((4, per, PLANES, rows + 2 * PAD, radial_count), f32),
            pltpu.VMEM((4, radial_count, radial_count), bf16),
            pltpu.VMEM((2, PLANES * rows, radial_count), bf16),
            pltpu.VMEM((2, PLANES // 2 * rows, radial_count), f32),
            pltpu.VMEM((3, per, 2, 4 * PLANES, radial_count), f32),
            pltpu.VMEM((3, per, 2, 4 * PLANES, radial_count), f32),
            dma((2,)),
            dma((2, per)),
            dma((per, PLANES - 1)),
            dma((per, PLANES - 1)),
            dma((per, PLANES - 1)),
            dma((per, PLANES - 1)),
            dma((3, per, 2)),
            dma((3, per, 2)),
        ],
        compiler_params=pltpu.CompilerParams(
            collective_id=0, has_side_effects=True, vmem_limit_bytes=40 << 20
        ),
    )(*[pltpu.with_memory_space_constraint(x, pltpu.HBM) for x in (field, courant.reshape(1, -1), table)])


def solution(mesh):
    size = mesh.shape["theta"]
    return jax.shard_map(
        functools.partial(body, size),
        mesh=mesh,
        in_specs=(P("gz", "theta", None), P()),
        out_specs=P("gz", "theta", None),
        check_vma=False,
    )
```
